256 devices in a mesh: dom: 16 (over z, x_lo), ref: 16 (over x_hi, y, core).
Axes of the slice: x: 4 (x_hi: 2, x_lo: 2; x = x_hi * 2 + x_lo), y: 4, z: 8, core: 2. Of those that a mesh axis runs over, the one named last changes fastest.
Arguments:
- particles: float32 [8192, 128], P('dom'), may hold values from -1.2 to 1.2
- references: float32 [16384, 128], P('ref'), may hold values from -1 to 1.2
Outputs:
- moved: float32 [8192, 128], P(('dom', 'ref'))
- drift: float32 [8192, 128], P(('dom', 'ref'))
The draws below stay inside these ranges and needn't reach their ends.
All inputs are finite; a program needn't handle non-finite values.
Results may differ from the reference program's by a relative error of at most 0.00035.
Values sent between devices are 32-bit elements; how exact they have to be, the bound alone decides.
A program may use at most 64 MiB of HBM per device.

```python
import jax
import jax.numpy as jnp
from jax import lax

D = 128
ROWS_DEV = 32
STEPS = 2
NPART = 8192
NREF = 16384
N_REF = 16


wide_count = 4


def wide_columns(key):
    order = jax.random.permutation(jax.random.fold_in(key, 7), D)
    return (order < wide_count).astype(jnp.float32)[None, :]


def draw_particles(key, part):
    column_mask = wide_columns(key)
    first_key, second_key = jax.random.split(jax.random.fold_in(key, 1))
    broad = jax.random.uniform(first_key, (NPART, D), jnp.float32, -1.0, 1.0)
    narrow = 0.08 * jax.random.truncated_normal(second_key, -5.0, 5.0, (NPART, D), jnp.float32)
    return column_mask * broad + (1.0 - column_mask) * narrow


def draw_references(key, part):
    column_mask = wide_columns(key)
    first_key, second_key = jax.random.split(jax.random.fold_in(key, 2))
    broad = jax.random.uniform(first_key, (NREF, D), jnp.float32, -0.8, 1.0)
    narrow = 0.06 * jax.random.truncated_normal(second_key, -5.0, 5.0, (NREF, D), jnp.float32)
    return column_mask * broad + (1.0 - column_mask) * narrow


def setup_inputs(seed: int = 0) -> dict:
    keys = jax.random.split(jax.random.key(seed), 3)
    particles = draw_particles(jax.random.fold_in(keys[2], 71), 0)
    references = draw_references(jax.random.fold_in(keys[2], 71), 0)
    return dict(particles=particles, references=references)


step_size = 0.5


def kernel_terms(block, others):
    inner = jnp.dot(block, others.T, precision=lax.Precision.HIGHEST, preferred_element_type=jnp.float32)
    squared = jnp.sum(block * block, axis=1)[:, None] + jnp.sum(others * others, axis=1)[None, :] - 2.0 * inner
    weights = jnp.exp(-0.5 * squared)
    pulled = jnp.dot(weights, others, precision=lax.Precision.HIGHEST, preferred_element_type=jnp.float32)
    return pulled, jnp.sum(weights, axis=1)


def reference(particles, references):
    count_p = particles.shape[0]
    count_r = references.shape[0]
    width = particles.shape[1]
    blocks = count_p // (ROWS_DEV * N_REF)
    current = particles
    for step in range(STEPS):
        def one_block(block):
            pull_p, sum_p = kernel_terms(block, current)
            pull_r, sum_r = kernel_terms(block, references)
            return (pull_p - sum_p[:, None] * block) / count_p - (pull_r - sum_r[:, None] * block) / count_r
        gradient = lax.map(one_block, current.reshape(blocks, count_p // blocks, width)).reshape(count_p, width)
        current = current - step_size * gradient
    return current, (current - particles) / step_size
```

```python
import math

import jax
import jax.numpy as jnp
from jax import lax
from jax.experimental import pallas as pl
from jax.experimental.pallas import tpu as pltpu
from jax.sharding import PartitionSpec as P

MESH = pl.DeviceIdType.MESH
F32, BF16 = jnp.float32, jnp.bfloat16
LOG2E = math.log2(math.e)

NDOM, NREFD = 16, 16
ROWS, WIDTH = 32, 128
BLOCK = ROWS * NREFD
REFS = 1024
STEP = 0.5
COUNT_P, COUNT_R = 8192, 16384

DOM_OFFSETS = [(z, x) for z in (4, 3, 5, 2, 6, 1, 7, 0) for x in (1, 0) if (z, x) != (0, 0)]
REF_OFFSETS = [
    (x, y, c) for x in (1, 0) for y in (2, 1, 3, 0) for c in (1, 0) if (x, y, c) != (0, 0, 0)
]


def dom_partner(d, offset):
    z, x = d // 2, d % 2
    return ((z + offset[0]) % 8) * 2 + (x + offset[1]) % 2


def ref_partner(r, offset):
    x, y, c = r // 8, (r // 2) % 4, r % 2
    return ((x + offset[0]) % 2) * 8 + ((y + offset[1]) % 4) * 2 + (c + offset[2]) % 2


def split(x):
    hi = x.astype(BF16)
    return hi, (x - hi.astype(F32)).astype(BF16)


def extra(norm, ones_first):
    lane = lax.broadcasted_iota(jnp.int32, (norm.shape[0], 128), 1)
    n1 = norm.astype(BF16).astype(F32)
    rest = norm - n1
    n2 = rest.astype(BF16).astype(F32)
    n3 = rest - n2
    at, one = (3, 0) if ones_first else (0, 3)
    out = jnp.where((lane >= one) & (lane < one + 3), 1.0, 0.0)
    out = jnp.where(lane == at, n1, out)
    out = jnp.where(lane == at + 1, n2, out)
    return jnp.where(lane == at + 2, n3, out).astype(BF16)


def source_operand(x):
    hi, lo = split(x)
    norm = jnp.sum(x * x, axis=1, keepdims=True) * (-0.5 * LOG2E)
    return jnp.concatenate([hi, lo, hi, extra(norm, False)], axis=1)


def target_operand(x):
    hi, lo = split(x * LOG2E)
    norm = jnp.sum(x * x, axis=1, keepdims=True) * (-0.5 * LOG2E)
    return jnp.concatenate([hi, hi, lo, extra(norm, True)], axis=1)


def pair_terms(a, s_ref, start, size):
    src = s_ref[pl.ds(start, size), :]
    expo = lax.dot_general(a, src, (((1,), (1,)), ((), ())), preferred_element_type=F32)
    w = jnp.exp2(expo)
    w_hi = w.astype(BF16)
    w_lo = (w - w_hi.astype(F32)).astype(BF16)
    one = jnp.dot(w_hi, src[:, :256], preferred_element_type=F32)
    two = jnp.dot(w_lo, src[:, :128], preferred_element_type=F32)
    sums = w[:, :128]
    for c in range(1, size // 128):
        sums = sums + w[:, c * 128 : (c + 1) * 128]
    return one[:, :128] + one[:, 128:] + two, sums


def kernel(
    p_hbm, r_hbm, moved_ref, drift_ref,
    p_v, r_v, aop, rop, sop, grad, lanes, part, own, g_b, g_a, rs,
    in_sem, b_send, b_recv, a_send, a_recv, rs_send, rs_recv,
):
    d, r = lax.axis_index("dom"), lax.axis_index("ref")
    copy_p = pltpu.make_async_copy(p_hbm, p_v, in_sem.at[0])
    copy_r = pltpu.make_async_copy(r_hbm, r_v, in_sem.at[1])
    copy_p.start()
    copy_r.start()

    barrier = pltpu.get_barrier_semaphore()
    for off in DOM_OFFSETS:
        pl.semaphore_signal(barrier, 1, device_id={"dom": dom_partner(d, off)}, device_id_type=MESH)
    for off in REF_OFFSETS:
        pl.semaphore_signal(barrier, 1, device_id={"ref": ref_partner(r, off)}, device_id_type=MESH)

    def b_copy(step, src, off):
        q = dom_partner(d, off)
        send = pltpu.make_async_remote_copy(
            src, g_b.at[step, d], b_send.at[step, q], b_recv.at[step, d],
            device_id={"dom": q}, device_id_type=MESH,
        )
        recv = pltpu.make_async_remote_copy(
            src, g_b.at[step, q], b_send.at[step, q], b_recv.at[step, q],
            device_id={"dom": q}, device_id_type=MESH,
        )
        return q, send, recv

    def a_copy(src, off):
        q = ref_partner(r, off)
        send = pltpu.make_async_remote_copy(
            src, g_a.at[r], a_send.at[q], a_recv.at[r],
            device_id={"ref": q}, device_id_type=MESH,
        )
        recv = pltpu.make_async_remote_copy(
            src, g_a.at[q], a_send.at[q], a_recv.at[q],
            device_id={"ref": q}, device_id_type=MESH,
        )
        return q, send, recv

    def rs_copy(step, off):
        q = ref_partner(r, off)
        send = pltpu.make_async_remote_copy(
            part.at[step, q], rs.at[step, r], rs_send.at[step, q], rs_recv.at[step, r],
            device_id={"ref": q}, device_id_type=MESH,
        )
        recv = pltpu.make_async_remote_copy(
            part.at[step, r], rs.at[step, q], rs_send.at[step, q], rs_recv.at[step, q],
            device_id={"ref": q}, device_id_type=MESH,
        )
        return q, send, recv

    def refs_part(rows):
        a = aop[rows, :]
        acc, sums = pair_terms(a, rop, 0, 512)
        acc2, sums2 = pair_terms(a, rop, 512, 512)
        grad[rows, :] = -0.5 * (acc + acc2)
        lanes[rows, :] = -0.5 * (sums + sums2)

    def particles_part(rows, x):
        acc, sums = pair_terms(aop[rows, :], sop, 0, 512)
        total = jnp.sum(lanes[rows, :] + sums, axis=1, keepdims=True)
        return grad[rows, :] + acc - total * x

    def half(i):
        return pl.ds(i * 256, 256)

    def exchange(step, x_of):
        for i in range(2):
            value = particles_part(half(i), x_of(i))
            part[step, pl.ds(i * 8, 8)] = value.reshape(8, ROWS, WIDTH)
        copies = [rs_copy(step, off) for off in REF_OFFSETS]
        for _, send, _ in copies:
            send.start()
        total = part[step, r]
        for q, _, recv in copies[::-1]:
            recv.wait_recv()
            total = total + rs[step, q]
        return total * (STEP / COUNT_P), [c[1] for c in copies]

    pending = []

    copy_p.wait()
    for i in range(2):
        aop[half(i), :] = target_operand(p_v[half(i), :])
    copy_r.wait()
    for i in range(4):
        rop[half(i), :] = source_operand(r_v[half(i), :])
    pl.semaphore_wait(barrier, len(DOM_OFFSETS) + len(REF_OFFSETS))
    mine = pl.ds(pl.multiple_of(r * ROWS, ROWS), ROWS)
    copies = [b_copy(0, p_v.at[mine], off) for off in DOM_OFFSETS]
    for _, send, _ in copies:
        send.start()
        pending.append(send)
    for i in range(2):
        refs_part(half(i))
    start = p_v[mine, :]
    sop[pl.ds(pl.multiple_of(d * ROWS, ROWS), ROWS), :] = source_operand(start)
    for q, _, recv in copies[::-1]:
        recv.wait_recv()
        sop[pl.ds(pl.multiple_of(q * ROWS, ROWS), ROWS), :] = source_operand(g_b[0, q])
    delta, sends = exchange(0, lambda i: p_v[half(i), :])
    pending += sends
    now = start - delta
    own[...] = now

    a_copies = [a_copy(own, off) for off in REF_OFFSETS]
    b_copies = [b_copy(1, own, off) for off in DOM_OFFSETS]
    for c in a_copies + b_copies:
        c[1].start()
        pending.append(c[1])
    g_a[r] = now
    aop[mine, :] = target_operand(now)
    sop[pl.ds(pl.multiple_of(d * ROWS, ROWS), ROWS), :] = source_operand(now)
    for q, _, recv in a_copies[::-1]:
        recv.wait_recv()
        aop[pl.ds(pl.multiple_of(q * ROWS, ROWS), ROWS), :] = target_operand(g_a[q])
    for i in range(2):
        refs_part(half(i))
    for q, _, recv in b_copies[::-1]:
        recv.wait_recv()
        sop[pl.ds(pl.multiple_of(q * ROWS, ROWS), ROWS), :] = source_operand(g_b[1, q])
    delta, sends = exchange(1, lambda i: g_a[pl.ds(i * 8, 8)].reshape(256, WIDTH))
    pending += sends
    final = now - delta
    moved_ref[...] = final
    drift_ref[...] = (final - start) * (1.0 / STEP)
    for send in pending:
        send.wait_send()


def on_device(particles, references):
    vmem = pl.BlockSpec(memory_space=pltpu.VMEM)
    anywhere = pl.BlockSpec(memory_space=pl.ANY)
    piece = jax.ShapeDtypeStruct((ROWS, WIDTH), F32)
    return pl.pallas_call(
        kernel,
        out_shape=(piece, piece),
        in_specs=[anywhere, anywhere],
        out_specs=(vmem, vmem),
        scratch_shapes=[
            pltpu.VMEM((BLOCK, WIDTH), F32),
            pltpu.VMEM((REFS, WIDTH), F32),
            pltpu.VMEM((BLOCK, 512), BF16),
            pltpu.VMEM((REFS, 512), BF16),
            pltpu.VMEM((NDOM * ROWS, 512), BF16),
            pltpu.VMEM((BLOCK, WIDTH), F32),
            pltpu.VMEM((BLOCK, WIDTH), F32),
            pltpu.VMEM((2, NREFD, ROWS, WIDTH), F32),
            pltpu.VMEM((ROWS, WIDTH), F32),
            pltpu.VMEM((2, NDOM, ROWS, WIDTH), F32),
            pltpu.VMEM((NREFD, ROWS, WIDTH), F32),
            pltpu.VMEM((2, NREFD, ROWS, WIDTH), F32),
            pltpu.SemaphoreType.DMA((2,)),
            pltpu.SemaphoreType.DMA((2, NDOM)),
            pltpu.SemaphoreType.DMA((2, NDOM)),
            pltpu.SemaphoreType.DMA((NREFD,)),
            pltpu.SemaphoreType.DMA((NREFD,)),
            pltpu.SemaphoreType.DMA((2, NREFD)),
            pltpu.SemaphoreType.DMA((2, NREFD)),
        ],
        compiler_params=pltpu.CompilerParams(collective_id=0, has_side_effects=True),
        name="flow",
    )(particles, references)


def solution(mesh):
    return jax.shard_map(
        on_device,
        mesh=mesh,
        in_specs=(P("dom", None), P("ref", None)),
        out_specs=(P(("dom", "ref"), None), P(("dom", "ref"), None)),
        check_vma=False,
    )
```

```python
import math

import jax
import jax.numpy as jnp
from jax import lax
from jax.experimental import pallas as pl
from jax.experimental.pallas import tpu as pltpu
from jax.sharding import PartitionSpec as P

MESH = pl.DeviceIdType.MESH
F32, BF16 = jnp.float32, jnp.bfloat16
LOG2E = math.log2(math.e)

NDOM, NREFD = 16, 16
ROWS, WIDTH = 32, 128
BLOCK = ROWS * NREFD
REFS = 1024
STEP = 0.5
COUNT_P, COUNT_R = 8192, 16384

DOM_SLOTS = [(0, 0), (0, 1), (1, 0), (7, 0), (1, 1), (7, 1), (2, 0), (6, 0)]
DOM_SLOTS += [(2, 1), (6, 1), (3, 0), (5, 0), (3, 1), (5, 1), (4, 0), (4, 1)]
REF_SLOTS = [(0, 0, 0), (0, 0, 1)] + [(0, y, c) for y in (1, 3, 2) for c in (0, 1)]
REF_SLOTS += [(1, y, c) for y in (0, 1, 3, 2) for c in (0, 1)]


def dom_partner(d, slot):
    dz, dx = DOM_SLOTS[slot]
    return ((d // 2 + dz) % 8) * 2 + (d % 2 + dx) % 2


def ref_partner(r, slot):
    dx, dy, dc = REF_SLOTS[slot]
    return ((r // 8 + dx) % 2) * 8 + (((r // 2) % 4 + dy) % 4) * 2 + (r % 2 + dc) % 2


def dom_back(slot):
    dz, dx = DOM_SLOTS[slot]
    return DOM_SLOTS.index((-dz % 8, dx))


def ref_back(slot):
    dx, dy, dc = REF_SLOTS[slot]
    return REF_SLOTS.index((dx, -dy % 4, dc))


def split(x):
    hi = x.astype(BF16)
    return hi, (x - hi.astype(F32)).astype(BF16)


def extra(norm, ones_first):
    lane = lax.broadcasted_iota(jnp.int32, (norm.shape[0], 128), 1)
    n1 = norm.astype(BF16).astype(F32)
    rest = norm - n1
    n2 = rest.astype(BF16).astype(F32)
    n3 = rest - n2
    at, one = (3, 0) if ones_first else (0, 3)
    out = jnp.where((lane >= one) & (lane < one + 3), 1.0, 0.0)
    out = jnp.where(lane == at, n1, out)
    out = jnp.where(lane == at + 1, n2, out)
    return jnp.where(lane == at + 2, n3, out).astype(BF16)


def source_operand(x):
    hi, lo = split(x)
    norm = jnp.sum(x * x, axis=1, keepdims=True) * (-0.5 * LOG2E)
    return jnp.concatenate([hi, lo, hi, extra(norm, False)], axis=1)


def target_operand(x):
    hi, lo = split(x * LOG2E)
    norm = jnp.sum(x * x, axis=1, keepdims=True) * (-0.5 * LOG2E)
    return jnp.concatenate([hi, hi, lo, extra(norm, True)], axis=1)


def pair_terms(a, s_ref, start, size):
    src = s_ref[pl.ds(start, size), :]
    expo = lax.dot_general(a, src, (((1,), (1,)), ((), ())), preferred_element_type=F32)
    w = jnp.exp2(expo)
    w_hi = w.astype(BF16)
    w_lo = (w - w_hi.astype(F32)).astype(BF16)
    one = jnp.dot(w_hi, src[:, :256], preferred_element_type=F32)
    two = jnp.dot(w_lo, src[:, :128], preferred_element_type=F32)
    sums = w[:, :128]
    for c in range(1, size // 128):
        sums = sums + w[:, c * 128 : (c + 1) * 128]
    return one[:, :128] + one[:, 128:] + two, sums


def kernel(
    p_hbm, r_hbm, out_ref,
    p_v, r_v, xs, aop, rop, sop, grad, lanes, part, own, g_b, g_a, rs,
    in_sem, b_send, b_recv, a_send, a_recv, rs_send, rs_recv,
):
    d, r = lax.axis_index("dom"), lax.axis_index("ref")
    mine = pl.ds(pl.multiple_of(r * ROWS, ROWS), ROWS)
    copy_own = pltpu.make_async_copy(p_hbm.at[mine], own.at[0], in_sem.at[0])
    copy_p = pltpu.make_async_copy(p_hbm, p_v, in_sem.at[1])
    copy_r = pltpu.make_async_copy(r_hbm, r_v, in_sem.at[2])
    copy_own.start()
    copy_p.start()
    copy_r.start()

    barrier = pltpu.get_barrier_semaphore()
    for slot in range(15, 0, -1):
        device = {"dom": dom_partner(d, slot)}
        pl.semaphore_signal(barrier, 1, device_id=device, device_id_type=MESH)
    for slot in range(15, 0, -1):
        device = {"ref": ref_partner(r, slot)}
        pl.semaphore_signal(barrier, 1, device_id=device, device_id_type=MESH)

    def dom_copy(src, dst, send, recv, slot, to):
        return pltpu.make_async_remote_copy(
            src, dst.at[to], send.at[slot], recv.at[to],
            device_id={"dom": dom_partner(d, slot)}, device_id_type=MESH,
        )

    def ref_copy(src, dst, send, recv, slot, to):
        return pltpu.make_async_remote_copy(
            src, dst.at[to], send.at[slot], recv.at[to],
            device_id={"ref": ref_partner(r, slot)}, device_id_type=MESH,
        )

    pending = []

    def send_b(step):
        for slot in range(15, 0, -1):
            args = own.at[step], g_b.at[step], b_send.at[step], b_recv.at[step]
            copy = dom_copy(*args, slot, dom_back(slot))
            copy.start()
            pending.append(copy)

    def wait_b(step, slots):
        for slot in slots:
            args = own.at[step], g_b.at[step], b_send.at[step], b_recv.at[step]
            dom_copy(*args, slot, slot).wait_recv()

    def send_a():
        for slot in range(15, 0, -1):
            copy = ref_copy(own.at[1], g_a, a_send, a_recv, slot, ref_back(slot))
            copy.start()
            pending.append(copy)

    def wait_a(slots):
        for slot in slots:
            ref_copy(own.at[1], g_a, a_send, a_recv, slot, slot).wait_recv()

    def send_rs(step, slots):
        for slot in slots:
            args = part.at[step, slot], rs.at[step], rs_send.at[step], rs_recv.at[step]
            copy = ref_copy(*args, slot, ref_back(slot))
            copy.start()
            pending.append(copy)

    def wait_rs(step):
        for slot in range(1, 16):
            args = part.at[step, slot], rs.at[step], rs_send.at[step], rs_recv.at[step]
            ref_copy(*args, slot, slot).wait_recv()
        total = part[step, 0] + rs[step, 1]
        for slot in range(2, 16):
            total = total + rs[step, slot]
        return total * (STEP / COUNT_P)

    near, far = pl.ds(0, 256), pl.ds(256, 256)

    def refs_part(rows):
        a = aop[rows, :]
        acc, sums = pair_terms(a, rop, 0, 512)
        acc2, sums2 = pair_terms(a, rop, 512, 512)
        grad[rows, :] = -0.5 * (acc + acc2)
        lanes[rows, :] = -0.5 * (sums + sums2)

    def near_part(rows):
        acc, sums = pair_terms(aop[rows, :], sop, 0, 256)
        grad[rows, :] += acc
        lanes[rows, :] += sums

    def far_part(step, rows):
        acc, sums = pair_terms(aop[rows, :], sop, 256, 256)
        total = jnp.sum(lanes[rows, :] + sums, axis=1, keepdims=True)
        value = grad[rows, :] + acc - total * xs[rows, :]
        part[step, pl.ds(rows.start // ROWS, 8)] = value.reshape(8, ROWS, WIDTH)

    def prep_b(step, rows):
        pieces = g_b[step, pl.ds(rows.start // ROWS, 8)]
        sop[rows, :] = source_operand(pieces.reshape(256, WIDTH))

    def finish(step):
        wait_b(step, range(8, 16))
        prep_b(step, far)
        far_part(step, far)
        send_rs(step, range(15, 7, -1))
        far_part(step, near)
        send_rs(step, range(7, 0, -1))
        return wait_rs(step)

    copy_own.wait()
    pl.semaphore_wait(barrier, 30)
    send_b(0)
    start = own[0]
    g_b[0, 0] = start
    copy_p.wait()
    for slot in range(16):
        rows = pl.ds(pl.multiple_of(ref_partner(r, slot) * ROWS, ROWS), ROWS)
        xs[pl.ds(slot * ROWS, ROWS), :] = p_v[rows, :]
    for rows in (near, far):
        aop[rows, :] = target_operand(xs[rows, :])
    copy_r.wait()
    for i in range(4):
        rows = pl.ds(i * 256, 256)
        rop[rows, :] = source_operand(r_v[rows, :])
    for rows in (near, far):
        refs_part(rows)
    wait_b(0, range(1, 8))
    prep_b(0, near)
    for rows in (near, far):
        near_part(rows)
    now = start - finish(0)

    own[1] = now
    send_a()
    send_b(1)
    g_b[1, 0] = now
    g_a[0] = now
    wait_a(range(1, 8))
    xs[near, :] = g_a[pl.ds(0, 8)].reshape(256, WIDTH)
    aop[near, :] = target_operand(xs[near, :])
    refs_part(near)
    wait_b(1, range(1, 8))
    prep_b(1, near)
    near_part(near)
    wait_a(range(8, 16))
    xs[far, :] = g_a[pl.ds(8, 8)].reshape(256, WIDTH)
    aop[far, :] = target_operand(xs[far, :])
    refs_part(far)
    near_part(far)
    delta = finish(1)
    out_ref[0] = start
    out_ref[1] = now
    out_ref[2] = delta
    for copy in pending:
        copy.wait_send()


def on_device(particles, references):
    out = pl.pallas_call(
        kernel,
        out_shape=jax.ShapeDtypeStruct((3, ROWS, WIDTH), F32),
        in_specs=[pl.BlockSpec(memory_space=pl.ANY)] * 2,
        out_specs=pl.BlockSpec(memory_space=pltpu.VMEM),
        scratch_shapes=[
            pltpu.VMEM((BLOCK, WIDTH), F32),
            pltpu.VMEM((REFS, WIDTH), F32),
            pltpu.VMEM((BLOCK, WIDTH), F32),
            pltpu.VMEM((BLOCK, 512), BF16),
            pltpu.VMEM((REFS, 512), BF16),
            pltpu.VMEM((NDOM * ROWS, 512), BF16),
            pltpu.VMEM((BLOCK, WIDTH), F32),
            pltpu.VMEM((BLOCK, WIDTH), F32),
            pltpu.VMEM((2, NREFD, ROWS, WIDTH), F32),
            pltpu.VMEM((2, ROWS, WIDTH), F32),
            pltpu.VMEM((2, NDOM, ROWS, WIDTH), F32),
            pltpu.VMEM((NREFD, ROWS, WIDTH), F32),
            pltpu.VMEM((2, NREFD, ROWS, WIDTH), F32),
            pltpu.SemaphoreType.DMA((3,)),
            pltpu.SemaphoreType.DMA((2, NDOM)),
            pltpu.SemaphoreType.DMA((2, NDOM)),
            pltpu.SemaphoreType.DMA((NREFD,)),
            pltpu.SemaphoreType.DMA((NREFD,)),
            pltpu.SemaphoreType.DMA((2, NREFD)),
            pltpu.SemaphoreType.DMA((2, NREFD)),
        ],
        compiler_params=pltpu.CompilerParams(collective_id=0, has_side_effects=True),
        name="flow",
    )(particles, references)
    moved = out[1] - out[2]
    return moved, (moved - out[0]) * (1.0 / STEP)


def solution(mesh):
    return jax.shard_map(
        on_device,
        mesh=mesh,
        in_specs=(P("dom", None), P("ref", None)),
        out_specs=(P(("dom", "ref"), None), P(("dom", "ref"), None)),
        check_vma=False,
    )
```

```python
import math

import jax
import jax.numpy as jnp
from jax import lax
from jax.experimental import pallas as pl
from jax.experimental.pallas import tpu as pltpu
from jax.sharding import PartitionSpec as P

MESH = pl.DeviceIdType.MESH
F32, BF16 = jnp.float32, jnp.bfloat16
LOG2E = math.log2(math.e)

NDOM, NREFD = 16, 16
ROWS, WIDTH = 32, 128
BLOCK = ROWS * NREFD
REFS = 1024
STEP = 0.5
COUNT_P, COUNT_R = 8192, 16384

DOM_SLOTS = [(0, 0), (0, 1), (1, 0), (7, 0), (1, 1), (7, 1), (2, 0), (6, 0)]
DOM_SLOTS += [(2, 1), (6, 1), (3, 0), (5, 0), (3, 1), (5, 1), (4, 0), (4, 1)]
REF_SLOTS = [(0, 0, 0), (0, 0, 1)] + [(0, y, c) for y in (1, 3, 2) for c in (0, 1)]
REF_SLOTS += [(1, y, c) for y in (0, 1, 3, 2) for c in (0, 1)]


def dom_partner(d, slot):
    dz, dx = DOM_SLOTS[slot]
    return ((d // 2 + dz) % 8) * 2 + (d % 2 + dx) % 2


def ref_partner(r, slot):
    dx, dy, dc = REF_SLOTS[slot]
    return ((r // 8 + dx) % 2) * 8 + (((r // 2) % 4 + dy) % 4) * 2 + (r % 2 + dc) % 2


def dom_back(slot):
    dz, dx = DOM_SLOTS[slot]
    return DOM_SLOTS.index((-dz % 8, dx))


def ref_back(slot):
    dx, dy, dc = REF_SLOTS[slot]
    return REF_SLOTS.index((dx, -dy % 4, dc))


def split(x):
    hi = x.astype(BF16)
    return hi, (x - hi.astype(F32)).astype(BF16)


def extra(norm, ones_first):
    lane = lax.broadcasted_iota(jnp.int32, (norm.shape[0], 128), 1)
    n1 = norm.astype(BF16).astype(F32)
    rest = norm - n1
    n2 = rest.astype(BF16).astype(F32)
    n3 = rest - n2
    at, one = (3, 0) if ones_first else (0, 3)
    out = jnp.where((lane >= one) & (lane < one + 3), 1.0, 0.0)
    out = jnp.where(lane == at, n1, out)
    out = jnp.where(lane == at + 1, n2, out)
    return jnp.where(lane == at + 2, n3, out).astype(BF16)


def source_operand(x):
    hi, lo = split(x)
    norm = jnp.sum(x * x, axis=1, keepdims=True) * (-0.5 * LOG2E)
    return jnp.concatenate([hi, lo, hi, extra(norm, False)], axis=1)


def target_operand(x):
    hi, lo = split(x * LOG2E)
    norm = jnp.sum(x * x, axis=1, keepdims=True) * (-0.5 * LOG2E)
    return jnp.concatenate([hi, hi, lo, extra(norm, True)], axis=1)


def pair_terms(a, s_ref, start, size):
    src = s_ref[pl.ds(start, size), :]
    expo = lax.dot_general(a, src, (((1,), (1,)), ((), ())), preferred_element_type=F32)
    w = jnp.exp2(expo)
    w_hi = w.astype(BF16)
    w_lo = (w - w_hi.astype(F32)).astype(BF16)
    one = jnp.dot(w_hi, src[:, :256], preferred_element_type=F32)
    two = jnp.dot(w_lo, src[:, :128], preferred_element_type=F32)
    sums = w[:, :128]
    for c in range(1, size // 128):
        sums = sums + w[:, c * 128 : (c + 1) * 128]
    return one[:, :128] + one[:, 128:] + two, sums


def kernel(
    p_hbm, r_hbm, out_ref,
    p_v, r_v, xs, aop, rop, sop, grad, lanes, part, own, g_b, g_a, rs,
    in_sem, b_send, b_recv, a_send, a_recv, rs_send, rs_recv,
):
    d, r = lax.axis_index("dom"), lax.axis_index("ref")
    mine = pl.ds(pl.multiple_of(r * ROWS, ROWS), ROWS)
    copy_own = pltpu.make_async_copy(p_hbm.at[mine], own.at[0], in_sem.at[0])
    copy_p = pltpu.make_async_copy(p_hbm, p_v, in_sem.at[1])
    copy_r = pltpu.make_async_copy(r_hbm, r_v, in_sem.at[2])
    copy_own.start()
    copy_p.start()
    copy_r.start()

    barrier = pltpu.get_barrier_semaphore()
    for slot in range(15, 0, -1):
        device = {"dom": dom_partner(d, slot)}
        pl.semaphore_signal(barrier, 1, device_id=device, device_id_type=MESH)
    for slot in range(15, 0, -1):
        device = {"ref": ref_partner(r, slot)}
        pl.semaphore_signal(barrier, 1, device_id=device, device_id_type=MESH)

    def dom_copy(src, dst, send, recv, slot):
        to = dom_back(slot)
        return pltpu.make_async_remote_copy(
            src, dst.at[to], send, recv.at[to // 8],
            device_id={"dom": dom_partner(d, slot)}, device_id_type=MESH,
        )

    def ref_copy(src, dst, send, recv, slot):
        to = ref_back(slot)
        return pltpu.make_async_remote_copy(
            src, dst.at[to], send, recv.at[to // 8],
            device_id={"ref": ref_partner(r, slot)}, device_id_type=MESH,
        )

    def send_b(step):
        for slot in range(15, 0, -1):
            dom_copy(own.at[step], g_b.at[step], b_send.at[step], b_recv.at[step], slot).start()

    def send_a():
        for slot in range(15, 0, -1):
            ref_copy(own.at[1], g_a, a_send, a_recv, slot).start()

    def send_rs(step, slots):
        for slot in slots:
            src = part.at[step, slot]
            ref_copy(src, rs.at[step], rs_send.at[step], rs_recv.at[step], slot).start()

    def arrived(dst, recv, half):
        pieces = dst.at[pl.ds(1, 7)] if half == 0 else dst.at[pl.ds(8, 8)]
        pltpu.make_async_copy(pieces, pieces, recv.at[half]).wait()

    def sent(dst, send):
        pieces = dst.at[pl.ds(1, 15)]
        pltpu.make_async_copy(pieces, pieces, send).wait()

    near, far = pl.ds(0, 256), pl.ds(256, 256)

    def refs_part(rows):
        a = aop[rows, :]
        acc, sums = pair_terms(a, rop, 0, 512)
        acc2, sums2 = pair_terms(a, rop, 512, 512)
        grad[rows, :] = -0.5 * (acc + acc2)
        lanes[rows, :] = -0.5 * (sums + sums2)

    def particles_part(step, rows):
        acc, sums = pair_terms(aop[rows, :], sop, 0, 512)
        total = jnp.sum(lanes[rows, :] + sums, axis=1, keepdims=True)
        value = grad[rows, :] + acc - total * xs[rows, :]
        count = rows.size // ROWS
        part[step, pl.ds(rows.start // ROWS, count)] = value.reshape(count, ROWS, WIDTH)

    def prep_b(step, rows):
        pieces = g_b[step, pl.ds(rows.start // ROWS, 8)]
        sop[rows, :] = source_operand(pieces.reshape(256, WIDTH))

    def finish(step):
        arrived(g_b.at[step], b_recv.at[step], 1)
        prep_b(step, far)
        arrived(g_b.at[step], b_recv.at[step], 0)
        prep_b(step, near)
        particles_part(step, far)
        send_rs(step, range(15, 7, -1))
        particles_part(step, near)
        send_rs(step, range(7, 0, -1))
        arrived(rs.at[step], rs_recv.at[step], 0)
        arrived(rs.at[step], rs_recv.at[step], 1)
        total = part[step, 0]
        for slot in range(1, 16):
            total = total + rs[step, slot]
        return total * (STEP / COUNT_P)

    copy_own.wait()
    pl.semaphore_wait(barrier, 30)
    send_b(0)
    start = own[0]
    g_b[0, 0] = start
    copy_p.wait()
    for slot in range(16):
        rows = pl.ds(pl.multiple_of(ref_partner(r, slot) * ROWS, ROWS), ROWS)
        xs[pl.ds(slot * ROWS, ROWS), :] = p_v[rows, :]
    for rows in (near, far):
        aop[rows, :] = target_operand(xs[rows, :])
    copy_r.wait()
    for i in range(4):
        rows = pl.ds(i * 256, 256)
        rop[rows, :] = source_operand(r_v[rows, :])
    for rows in (near, far):
        refs_part(rows)
    now = start - finish(0)

    own[1] = now
    send_a()
    send_b(1)
    g_b[1, 0] = now
    g_a[0] = now
    for half, rows in ((0, near), (1, far)):
        arrived(g_a, a_recv, half)
        xs[rows, :] = g_a[pl.ds(half * 8, 8)].reshape(256, WIDTH)
        aop[rows, :] = target_operand(xs[rows, :])
        refs_part(rows)
    delta = finish(1)
    out_ref[0] = start
    out_ref[1] = now
    out_ref[2] = delta
    for step in range(2):
        sent(g_b.at[step], b_send.at[step])
        sent(rs.at[step], rs_send.at[step])
    sent(g_a, a_send)


def on_device(particles, references):
    inputs = [pltpu.with_memory_space_constraint(x, pltpu.HBM) for x in (particles, references)]
    out = pl.pallas_call(
        kernel,
        out_shape=jax.ShapeDtypeStruct((3, ROWS, WIDTH), F32),
        in_specs=[pl.BlockSpec(memory_space=pltpu.HBM)] * 2,
        out_specs=pl.BlockSpec(memory_space=pltpu.VMEM),
        scratch_shapes=[
            pltpu.VMEM((BLOCK, WIDTH), F32),
            pltpu.VMEM((REFS, WIDTH), F32),
            pltpu.VMEM((BLOCK, WIDTH), F32),
            pltpu.VMEM((BLOCK, 512), BF16),
            pltpu.VMEM((REFS, 512), BF16),
            pltpu.VMEM((NDOM * ROWS, 512), BF16),
            pltpu.VMEM((BLOCK, WIDTH), F32),
            pltpu.VMEM((BLOCK, WIDTH), F32),
            pltpu.VMEM((2, NREFD, ROWS, WIDTH), F32),
            pltpu.VMEM((2, ROWS, WIDTH), F32),
            pltpu.VMEM((2, NDOM, ROWS, WIDTH), F32),
            pltpu.VMEM((NREFD, ROWS, WIDTH), F32),
            pltpu.VMEM((2, NREFD, ROWS, WIDTH), F32),
            pltpu.SemaphoreType.DMA((3,)),
            pltpu.SemaphoreType.DMA((2,)),
            pltpu.SemaphoreType.DMA((2, 2)),
            pltpu.SemaphoreType.DMA(()),
            pltpu.SemaphoreType.DMA((2,)),
            pltpu.SemaphoreType.DMA((2,)),
            pltpu.SemaphoreType.DMA((2, 2)),
        ],
        compiler_params=pltpu.CompilerParams(
            collective_id=0, has_side_effects=True, vmem_limit_bytes=24 << 20
        ),
        name="flow",
    )(*inputs)
    moved = out[1] - out[2]
    return moved, (moved - out[0]) * (1.0 / STEP)


def solution(mesh):
    return jax.shard_map(
        on_device,
        mesh=mesh,
        in_specs=(P("dom", None), P("ref", None)),
        out_specs=(P(("dom", "ref"), None), P(("dom", "ref"), None)),
        check_vma=False,
    )
```

```python
import math

import jax
import jax.numpy as jnp
from jax import lax
from jax.experimental import pallas as pl
from jax.experimental.pallas import tpu as pltpu
from jax.sharding import PartitionSpec as P

MESH = pl.DeviceIdType.MESH
F32, BF16 = jnp.float32, jnp.bfloat16
LOG2E = math.log2(math.e)

NDOM, NREFD = 16, 16
ROWS, WIDTH = 32, 128
BLOCK = ROWS * NREFD
REFS = 1024
STEP = 0.5
COUNT_P, COUNT_R = 8192, 16384

DZ = (0, 1, 7, 2, 6, 3, 5, 4)
DOM_SLOTS = [(dz, dx) for dz in DZ for dx in (0, 1)]
REF_SLOTS = [(0, 0, 0), (0, 0, 1)] + [(0, y, c) for y in (1, 3, 2) for c in (0, 1)]
REF_SLOTS += [(1, y, c) for y in (0, 1, 3, 2) for c in (0, 1)]
NOWHERE = 4.0


def dom_partner(d, slot):
    dz, dx = DOM_SLOTS[slot]
    return ((d // 2 + dz) % 8) * 2 + (d % 2 + dx) % 2


def ref_partner(r, slot):
    dx, dy, dc = REF_SLOTS[slot]
    return ((r // 8 + dx) % 2) * 8 + (((r // 2) % 4 + dy) % 4) * 2 + (r % 2 + dc) % 2


def dom_back(slot):
    dz, dx = DOM_SLOTS[slot]
    return DOM_SLOTS.index((-dz % 8, dx))


def ref_back(slot):
    dx, dy, dc = REF_SLOTS[slot]
    return REF_SLOTS.index((dx, -dy % 4, dc))


def dom_rank(d):
    z = d // 2
    return (z * (8 - z) * 8 + z) * 2 + d % 2


def ref_rank(r):
    y = (r // 2) % 4
    return (y * (4 - y) + 4 * (r // 8)) * 16 + r


def split(x):
    hi = x.astype(BF16)
    return hi, (x - hi.astype(F32)).astype(BF16)


def extra(norm, ones_first):
    lane = lax.broadcasted_iota(jnp.int32, (norm.shape[0], 128), 1)
    n1 = norm.astype(BF16).astype(F32)
    rest = norm - n1
    n2 = rest.astype(BF16).astype(F32)
    n3 = rest - n2
    at, one = (3, 0) if ones_first else (0, 3)
    out = jnp.where((lane >= one) & (lane < one + 3), 1.0, 0.0)
    out = jnp.where(lane == at, n1, out)
    out = jnp.where(lane == at + 1, n2, out)
    return jnp.where(lane == at + 2, n3, out).astype(BF16)


def source_operand(x):
    hi, lo = split(x)
    norm = jnp.sum(x * x, axis=1, keepdims=True) * (-0.5 * LOG2E)
    return jnp.concatenate([hi, lo, hi, extra(norm, False)], axis=1)


def target_operand(x):
    hi, lo = split(x * LOG2E)
    norm = jnp.sum(x * x, axis=1, keepdims=True) * (-0.5 * LOG2E)
    return jnp.concatenate([hi, hi, lo, extra(norm, True)], axis=1)


def pair_terms(a, s_ref, start, size):
    src = s_ref[pl.ds(start, size), :]
    expo = lax.dot_general(a, src, (((1,), (1,)), ((), ())), preferred_element_type=F32)
    w = jnp.exp2(expo)
    w_hi = w.astype(BF16)
    w_lo = (w - w_hi.astype(F32)).astype(BF16)
    one = jnp.dot(w_hi, src[:, :256], preferred_element_type=F32)
    two = jnp.dot(w_lo, src[:, :128], preferred_element_type=F32)
    sums = w[:, :128]
    for c in range(1, size // 128):
        sums = sums + w[:, c * 128 : (c + 1) * 128]
    return one[:, :128] + one[:, 128:] + two, sums


def kernel(
    p_hbm, r_hbm, out_ref,
    p_v, r_v, xs, aop, rop, sop, bop, asop, grad, lanes, part, own, g_b, g_a, rs, back, g_back,
    in_sem, b_send, b_recv, back_send, back_recv, a_recv, ref_send, rs_recv, ready,
):
    d, r = lax.axis_index("dom"), lax.axis_index("ref")
    mine = pl.ds(pl.multiple_of(r * ROWS, ROWS), ROWS)
    copy_own = pltpu.make_async_copy(p_hbm.at[mine], own.at[0], in_sem.at[0])
    copy_p = pltpu.make_async_copy(p_hbm, p_v, in_sem.at[1])
    copy_r = pltpu.make_async_copy(r_hbm, r_v, in_sem.at[2])
    copy_own.start()
    copy_p.start()
    copy_r.start()

    rank = dom_rank(d)
    pairs = [(1, 1)] + [(2 * i, 2) for i in range(1, 8)]
    dom_later = [dom_rank(dom_partner(d, first)) > rank for first, _ in pairs]
    ref_later = [None] + [ref_rank(ref_partner(r, slot)) > ref_rank(r) for slot in range(1, 16)]
    n_dom = sum(jnp.where(later, 0, size) for later, (_, size) in zip(dom_later, pairs))
    n_ref = sum(jnp.where(later, 0, 1) for later in ref_later[1:])
    far_group = d // 2 * (8 - d // 2) < 14

    barrier = pltpu.get_barrier_semaphore()
    for i in (7, 6, 5, 4, 3, 2, 1, 0):
        first, size = pairs[i]

        @pl.when(dom_later[i])
        def _():
            for slot in range(first, first + size):
                device = {"dom": dom_partner(d, slot)}
                pl.semaphore_signal(barrier, 1, device_id=device, device_id_type=MESH)

    for slot in range(15, 0, -1):

        @pl.when(ref_later[slot])
        def _():
            device = {"ref": ref_partner(r, slot)}
            pl.semaphore_signal(barrier, 1, device_id=device, device_id_type=MESH)

    def dom_copy(src, dst, send, recv, slot):
        to = dom_back(slot)
        return pltpu.make_async_remote_copy(
            src, dst.at[to], send.at[slot // 2], recv.at[to // 2],
            device_id={"dom": dom_partner(d, slot)}, device_id_type=MESH,
        )

    def ref_copy(src, dst, recv, slot):
        to = ref_back(slot)
        return pltpu.make_async_remote_copy(
            src, dst.at[to], ref_send, recv.at[to // 8],
            device_id={"ref": ref_partner(r, slot)}, device_id_type=MESH,
        )

    def wait_bytes(pieces, sem):
        pltpu.make_async_copy(pieces, pieces, sem).wait()

    def send_b(step):
        for i in (7, 5, 6, 3, 4, 1, 2, 0):
            first, size = pairs[i]

            @pl.when(jnp.logical_not(dom_later[i]))
            def _():
                for slot in range(first + size - 1, first - 1, -1):
                    dom_copy(own.at[step], g_b.at[step], b_send, b_recv.at[step], slot).start()

    def send_back(step, group):
        for i in (3, 1, 2, 0) if group == 0 else (7, 5, 6, 4):
            first, size = pairs[i]

            @pl.when(dom_later[i])
            def _():
                for slot in range(first + size - 1, first - 1, -1):
                    src = back.at[step, slot]
                    dom_copy(src, g_back.at[step], back_send, back_recv.at[step], slot).start()

    def wait_b(step, group):
        for i in range(4 * group, 4 * group + 4):
            first, size = pairs[i]

            @pl.when(dom_later[i])
            def _():
                wait_bytes(g_b.at[step, pl.ds(first, size)], b_recv.at[step, first // 2])

    def wait_back(step):
        for i in range(8):
            first, size = pairs[i]

            @pl.when(jnp.logical_not(dom_later[i]))
            def _():
                wait_bytes(g_back.at[step, pl.ds(first, size)], back_recv.at[step, first // 2])

    def fill():
        for i in range(8):
            first, size = pairs[i]

            @pl.when(jnp.logical_not(dom_later[i]))
            def _():
                for step in range(2):
                    g_b[step, pl.ds(first, size)] = jnp.full((size, ROWS, WIDTH), NOWHERE, F32)

            @pl.when(dom_later[i])
            def _():
                for step in range(2):
                    g_back[step, pl.ds(first, size)] = jnp.zeros((size, ROWS, WIDTH), F32)

    def send_a():
        for slot in range(15, 0, -1):
            ref_copy(own.at[1], g_a, a_recv, slot).start()

    def arrived(dst, recv, half):
        wait_bytes(dst.at[pl.ds(1, 7)] if half == 0 else dst.at[pl.ds(8, 8)], recv.at[half])

    near, far = pl.ds(0, 256), pl.ds(256, 256)

    def refs_part(rows):
        a = aop[rows, :]
        acc, sums = pair_terms(a, rop, 0, 512)
        acc2, sums2 = pair_terms(a, rop, 512, 512)
        grad[rows, :] = -0.5 * (acc + acc2)
        lanes[rows, :] = -0.5 * (sums + sums2)

    def prep_a(rows):
        x = xs[rows, :]
        aop[rows, :] = target_operand(x)

    def prep_b(step, group):
        rows = near if group == 0 else far
        x = g_b[step, pl.ds(group * 8, 8)].reshape(256, WIDTH)
        sop[rows, :] = source_operand(x)
        bop[rows, :] = target_operand(x)

    def forward(group):
        for rows in (far, near):
            acc, sums = pair_terms(aop[rows, :], sop, group * 256, 256)
            grad[rows, :] += acc
            lanes[rows, :] += sums

    def reverse(step, group):
        rows, slots = (near, far)[group], pl.ds(group * 8, 8)
        acc, sums = pair_terms(bop[rows, :], asop, 0, 512)
        x = g_b[step, slots].reshape(256, WIDTH)
        value = acc - jnp.sum(sums, axis=1, keepdims=True) * x
        back[step, slots] = value.reshape(8, ROWS, WIDTH)

    def send_rs(step):
        for rows, slots, order in ((far, pl.ds(8, 8), range(15, 7, -1)), (near, pl.ds(0, 8), range(7, 0, -1))):
            total = jnp.sum(lanes[rows, :], axis=1, keepdims=True)
            value = grad[rows, :] - total * xs[rows, :]
            part[step, slots] = value.reshape(8, ROWS, WIDTH)
            for slot in order:
                ref_copy(part.at[step, slot], rs.at[step], rs_recv.at[step], slot).start()

    def finish(step):
        wait_b(step, 0)
        prep_b(step, 0)
        forward(0)
        reverse(step, 0)
        send_back(step, 0)

        @pl.when(far_group)
        def _():
            wait_b(step, 1)
            prep_b(step, 1)
            forward(1)

        if step == 0:

            @pl.when(n_ref < 15)
            def _():
                pl.semaphore_wait(ready, 15 - n_ref)

        send_rs(step)

        @pl.when(far_group)
        def _():
            reverse(step, 1)
            send_back(step, 1)

        arrived(rs.at[step], rs_recv.at[step], 0)
        arrived(rs.at[step], rs_recv.at[step], 1)
        total = part[step, 0]
        for slot in range(1, 16):
            total = total + rs[step, slot]
        wait_back(step)
        for slot in range(1, 16):
            total = total + g_back[step, slot]
        return total * (STEP / COUNT_P)

    copy_own.wait()

    @pl.when(n_dom + n_ref > 0)
    def _():
        pl.semaphore_wait(barrier, n_dom + n_ref)

    send_b(0)
    for slot in range(15, 0, -1):

        @pl.when(jnp.logical_not(ref_later[slot]))
        def _():
            device = {"ref": ref_partner(r, slot)}
            pl.semaphore_signal(ready, 1, device_id=device, device_id_type=MESH)

    start = own[0]
    g_b[0, 0] = start
    fill()
    copy_p.wait()
    for slot in range(16):
        rows = pl.ds(pl.multiple_of(ref_partner(r, slot) * ROWS, ROWS), ROWS)
        xs[pl.ds(slot * ROWS, ROWS), :] = p_v[rows, :]
    for rows in (near, far):
        aop[rows, :] = target_operand(xs[rows, :])
        asop[rows, :] = source_operand(xs[rows, :])
    copy_r.wait()
    for i in range(4):
        rows = pl.ds(i * 256, 256)
        rop[rows, :] = source_operand(r_v[rows, :])
    for rows in (near, far):
        refs_part(rows)
    now = start - finish(0)

    own[1] = now
    send_a()
    send_b(1)
    g_b[1, 0] = now
    g_a[0] = now
    for half, rows in ((0, near), (1, far)):
        arrived(g_a, a_recv, half)
        xs[rows, :] = g_a[pl.ds(half * 8, 8)].reshape(256, WIDTH)
        aop[rows, :] = target_operand(xs[rows, :])
        asop[rows, :] = source_operand(xs[rows, :])
        refs_part(rows)
    delta = finish(1)
    out_ref[0] = start
    out_ref[1] = now
    out_ref[2] = delta
    for i in range(8):
        first, size = pairs[i]

        @pl.when(dom_later[i])
        def _():
            wait_bytes(back.at[:, pl.ds(first, size)], back_send.at[first // 2])

        @pl.when(jnp.logical_not(dom_later[i]))
        def _():
            wait_bytes(g_b.at[:, pl.ds(first, size)], b_send.at[first // 2])

    wait_bytes(g_a.at[pl.ds(1, 15)], ref_send)
    for step in range(2):
        wait_bytes(rs.at[step, pl.ds(1, 15)], ref_send)


def on_device(particles, references):
    inputs = [pltpu.with_memory_space_constraint(x, pltpu.HBM) for x in (particles, references)]
    out = pl.pallas_call(
        kernel,
        out_shape=jax.ShapeDtypeStruct((3, ROWS, WIDTH), F32),
        in_specs=[pl.BlockSpec(memory_space=pltpu.HBM)] * 2,
        out_specs=pl.BlockSpec(memory_space=pltpu.VMEM),
        scratch_shapes=[
            pltpu.VMEM((BLOCK, WIDTH), F32),
            pltpu.VMEM((REFS, WIDTH), F32),
            pltpu.VMEM((BLOCK, WIDTH), F32),
            pltpu.VMEM((BLOCK, 512), BF16),
            pltpu.VMEM((REFS, 512), BF16),
            pltpu.VMEM((NDOM * ROWS, 512), BF16),
            pltpu.VMEM((NDOM * ROWS, 512), BF16),
            pltpu.VMEM((BLOCK, 512), BF16),
            pltpu.VMEM((BLOCK, WIDTH), F32),
            pltpu.VMEM((BLOCK, WIDTH), F32),
            pltpu.VMEM((2, NREFD, ROWS, WIDTH), F32),
            pltpu.VMEM((2, ROWS, WIDTH), F32),
            pltpu.VMEM((2, NDOM, ROWS, WIDTH), F32),
            pltpu.VMEM((NREFD, ROWS, WIDTH), F32),
            pltpu.VMEM((2, NREFD, ROWS, WIDTH), F32),
            pltpu.VMEM((2, NDOM, ROWS, WIDTH), F32),
            pltpu.VMEM((2, NDOM, ROWS, WIDTH), F32),
            pltpu.SemaphoreType.DMA((3,)),
            pltpu.SemaphoreType.DMA((8,)),
            pltpu.SemaphoreType.DMA((2, 8)),
            pltpu.SemaphoreType.DMA((8,)),
            pltpu.SemaphoreType.DMA((2, 8)),
            pltpu.SemaphoreType.DMA((2,)),
            pltpu.SemaphoreType.DMA(()),
            pltpu.SemaphoreType.DMA((2, 2)),
            pltpu.SemaphoreType.REGULAR,
        ],
        compiler_params=pltpu.CompilerParams(
            collective_id=0, has_side_effects=True, vmem_limit_bytes=24 << 20
        ),
        name="flow",
    )(*inputs)
    moved = out[1] - out[2]
    return moved, (moved - out[0]) * (1.0 / STEP)


def solution(mesh):
    return jax.shard_map(
        on_device,
        mesh=mesh,
        in_specs=(P("dom", None), P("ref", None)),
        out_specs=(P(("dom", "ref"), None), P(("dom", "ref"), None)),
        check_vma=False,
    )
```

```python
import math

import jax
import jax.numpy as jnp
from jax import lax
from jax.experimental import pallas as pl
from jax.experimental.pallas import tpu as pltpu
from jax.sharding import PartitionSpec as P

MESH = pl.DeviceIdType.MESH
F32, BF16 = jnp.float32, jnp.bfloat16
LOG2E = math.log2(math.e)

NDOM, NREFD = 16, 16
ROWS, WIDTH = 32, 128
BLOCK = ROWS * NREFD
REFS = 1024
STEP = 0.5
COUNT_P, COUNT_R = 8192, 16384

DOM_SLOTS = [(0, 0), (0, 1), (1, 0), (7, 0), (1, 1), (7, 1), (2, 0), (6, 0)]
DOM_SLOTS += [(2, 1), (6, 1), (3, 0), (5, 0), (3, 1), (5, 1), (4, 0), (4, 1)]
REF_SLOTS = [(0, 0, 0), (0, 0, 1)] + [(0, y, c) for y in (1, 3, 2) for c in (0, 1)]
REF_SLOTS += [(1, y, c) for y in (0, 1, 3, 2) for c in (0, 1)]


def dom_partner(d, slot):
    dz, dx = DOM_SLOTS[slot]
    return ((d // 2 + dz) % 8) * 2 + (d % 2 + dx) % 2


def ref_partner(r, slot):
    dx, dy, dc = REF_SLOTS[slot]
    return ((r // 8 + dx) % 2) * 8 + (((r // 2) % 4 + dy) % 4) * 2 + (r % 2 + dc) % 2


def dom_back(slot):
    dz, dx = DOM_SLOTS[slot]
    return DOM_SLOTS.index((-dz % 8, dx))


def ref_back(slot):
    dx, dy, dc = REF_SLOTS[slot]
    return REF_SLOTS.index((dx, -dy % 4, dc))


def split(x):
    hi = x.astype(BF16)
    return hi, (x - hi.astype(F32)).astype(BF16)


def extra(norm, ones_first):
    lane = lax.broadcasted_iota(jnp.int32, (norm.shape[0], 128), 1)
    n1 = norm.astype(BF16).astype(F32)
    rest = norm - n1
    n2 = rest.astype(BF16).astype(F32)
    n3 = rest - n2
    at, one = (3, 0) if ones_first else (0, 3)
    out = jnp.where((lane >= one) & (lane < one + 3), 1.0, 0.0)
    out = jnp.where(lane == at, n1, out)
    out = jnp.where(lane == at + 1, n2, out)
    return jnp.where(lane == at + 2, n3, out).astype(BF16)


def source_operand(x):
    hi, lo = split(x)
    norm = jnp.sum(x * x, axis=1, keepdims=True) * (-0.5 * LOG2E)
    return jnp.concatenate([hi, lo, hi, extra(norm, False)], axis=1)


def target_operand(x):
    hi, lo = split(x * LOG2E)
    norm = jnp.sum(x * x, axis=1, keepdims=True) * (-0.5 * LOG2E)
    return jnp.concatenate([hi, hi, lo, extra(norm, True)], axis=1)


def pair_terms(a, s_ref, start, size):
    src = s_ref[pl.ds(start, size), :]
    expo = lax.dot_general(a, src, (((1,), (1,)), ((), ())), preferred_element_type=F32)
    w = jnp.exp2(expo)
    w_hi = w.astype(BF16)
    w_lo = (w - w_hi.astype(F32)).astype(BF16)
    one = jnp.dot(w_hi, src[:, :256], preferred_element_type=F32)
    two = jnp.dot(w_lo, src[:, :128], preferred_element_type=F32)
    sums = w[:, :128]
    for c in range(1, size // 128):
        sums = sums + w[:, c * 128 : (c + 1) * 128]
    return one[:, :128] + one[:, 128:] + two, sums


def kernel(
    p_hbm, r_hbm, out_ref,
    p_v, r_v, xs, aop, rop, sop, grad, lanes, part, own, g_b, g_a, rs,
    in_sem, b_send, b_recv, a_send, a_recv, rs_send, rs_recv,
):
    d, r = lax.axis_index("dom"), lax.axis_index("ref")
    mine = pl.ds(pl.multiple_of(r * ROWS, ROWS), ROWS)
    copy_own = pltpu.make_async_copy(p_hbm.at[mine], own.at[0], in_sem.at[0])
    copy_p = pltpu.make_async_copy(p_hbm, p_v, in_sem.at[1])
    copy_r = pltpu.make_async_copy(r_hbm, r_v, in_sem.at[2])
    copy_own.start()
    copy_p.start()
    copy_r.start()

    barrier = pltpu.get_barrier_semaphore()
    for slot in range(15, 0, -1):
        device = {"dom": dom_partner(d, slot)}
        pl.semaphore_signal(barrier, 1, device_id=device, device_id_type=MESH)
    for slot in range(15, 0, -1):
        device = {"ref": ref_partner(r, slot)}
        pl.semaphore_signal(barrier, 1, device_id=device, device_id_type=MESH)

    def dom_copy(src, dst, send, recv, slot):
        to = dom_back(slot)
        return pltpu.make_async_remote_copy(
            src, dst.at[to], send, recv.at[to // 8],
            device_id={"dom": dom_partner(d, slot)}, device_id_type=MESH,
        )

    def ref_copy(src, dst, send, recv, slot):
        to = ref_back(slot)
        return pltpu.make_async_remote_copy(
            src, dst.at[to], send, recv.at[to // 8],
            device_id={"ref": ref_partner(r, slot)}, device_id_type=MESH,
        )

    def send_b(step):
        first = [s for x in (1, 0) for s in range(15, 0, -1) if DOM_SLOTS[s][1] == x]
        for slot in range(15, 0, -1) if step else first:
            dom_copy(own.at[step], g_b.at[step], b_send.at[step], b_recv.at[step], slot).start()

    def send_a():
        for slot in range(15, 0, -1):
            ref_copy(own.at[1], g_a, a_send, a_recv, slot).start()

    def send_rs(step, slots):
        for slot in slots:
            src = part.at[step, slot]
            ref_copy(src, rs.at[step], rs_send.at[step], rs_recv.at[step], slot).start()

    def arrived(dst, recv, half):
        pieces = dst.at[pl.ds(1, 7)] if half == 0 else dst.at[pl.ds(8, 8)]
        pltpu.make_async_copy(pieces, pieces, recv.at[half]).wait()

    def sent(dst, send):
        pieces = dst.at[pl.ds(1, 15)]
        pltpu.make_async_copy(pieces, pieces, send).wait()

    near, far = pl.ds(0, 256), pl.ds(256, 256)

    def refs_part(rows):
        a = aop[rows, :]
        acc, sums = pair_terms(a, rop, 0, 512)
        acc2, sums2 = pair_terms(a, rop, 512, 512)
        grad[rows, :] = -0.5 * (acc + acc2)
        lanes[rows, :] = -0.5 * (sums + sums2)

    def particles_part(step, rows):
        acc, sums = pair_terms(aop[rows, :], sop, 0, 512)
        total = jnp.sum(lanes[rows, :] + sums, axis=1, keepdims=True)
        value = grad[rows, :] + acc - total * xs[rows, :]
        count = rows.size // ROWS
        part[step, pl.ds(rows.start // ROWS, count)] = value.reshape(count, ROWS, WIDTH)

    def prep_b(step, rows):
        pieces = g_b[step, pl.ds(rows.start // ROWS, 8)]
        sop[rows, :] = source_operand(pieces.reshape(256, WIDTH))

    def finish(step):
        arrived(g_b.at[step], b_recv.at[step], 1)
        prep_b(step, far)
        arrived(g_b.at[step], b_recv.at[step], 0)
        prep_b(step, near)
        particles_part(step, far)
        send_rs(step, range(15, 7, -1))
        particles_part(step, near)
        send_rs(step, range(7, 0, -1))
        arrived(rs.at[step], rs_recv.at[step], 0)
        arrived(rs.at[step], rs_recv.at[step], 1)
        total = part[step, 0]
        for slot in range(1, 16):
            total = total + rs[step, slot]
        return total * (STEP / COUNT_P)

    copy_own.wait()
    pl.semaphore_wait(barrier, 30)
    send_b(0)
    start = own[0]
    g_b[0, 0] = start
    copy_p.wait()
    for slot in range(16):
        rows = pl.ds(pl.multiple_of(ref_partner(r, slot) * ROWS, ROWS), ROWS)
        xs[pl.ds(slot * ROWS, ROWS), :] = p_v[rows, :]
    for rows in (near, far):
        aop[rows, :] = target_operand(xs[rows, :])
    copy_r.wait()
    for i in range(4):
        rows = pl.ds(i * 256, 256)
        rop[rows, :] = source_operand(r_v[rows, :])
    for rows in (near, far):
        refs_part(rows)
    now = start - finish(0)

    own[1] = now
    send_a()
    send_b(1)
    g_b[1, 0] = now
    g_a[0] = now
    for half, rows in ((0, near), (1, far)):
        arrived(g_a, a_recv, half)
        xs[rows, :] = g_a[pl.ds(half * 8, 8)].reshape(256, WIDTH)
        aop[rows, :] = target_operand(xs[rows, :])
        refs_part(rows)
    delta = finish(1)
    out_ref[0] = start
    out_ref[1] = now
    out_ref[2] = delta
    for step in range(2):
        sent(g_b.at[step], b_send.at[step])
        sent(rs.at[step], rs_send.at[step])
    sent(g_a, a_send)


def on_device(particles, references):
    inputs = [pltpu.with_memory_space_constraint(x, pltpu.HBM) for x in (particles, references)]
    out = pl.pallas_call(
        kernel,
        out_shape=jax.ShapeDtypeStruct((3, ROWS, WIDTH), F32),
        in_specs=[pl.BlockSpec(memory_space=pltpu.HBM)] * 2,
        out_specs=pl.BlockSpec(memory_space=pltpu.VMEM),
        scratch_shapes=[
            pltpu.VMEM((BLOCK, WIDTH), F32),
            pltpu.VMEM((REFS, WIDTH), F32),
            pltpu.VMEM((BLOCK, WIDTH), F32),
            pltpu.VMEM((BLOCK, 512), BF16),
            pltpu.VMEM((REFS, 512), BF16),
            pltpu.VMEM((NDOM * ROWS, 512), BF16),
            pltpu.VMEM((BLOCK, WIDTH), F32),
            pltpu.VMEM((BLOCK, WIDTH), F32),
            pltpu.VMEM((2, NREFD, ROWS, WIDTH), F32),
            pltpu.VMEM((2, ROWS, WIDTH), F32),
            pltpu.VMEM((2, NDOM, ROWS, WIDTH), F32),
            pltpu.VMEM((NREFD, ROWS, WIDTH), F32),
            pltpu.VMEM((2, NREFD, ROWS, WIDTH), F32),
            pltpu.SemaphoreType.DMA((3,)),
            pltpu.SemaphoreType.DMA((2,)),
            pltpu.SemaphoreType.DMA((2, 2)),
            pltpu.SemaphoreType.DMA(()),
            pltpu.SemaphoreType.DMA((2,)),
            pltpu.SemaphoreType.DMA((2,)),
            pltpu.SemaphoreType.DMA((2, 2)),
        ],
        compiler_params=pltpu.CompilerParams(
            collective_id=0, has_side_effects=True, vmem_limit_bytes=24 << 20
        ),
        name="flow",
    )(*inputs)
    moved = out[1] - out[2]
    return moved, (moved - out[0]) * (1.0 / STEP)


def solution(mesh):
    return jax.shard_map(
        on_device,
        mesh=mesh,
        in_specs=(P("dom", None), P("ref", None)),
        out_specs=(P(("dom", "ref"), None), P(("dom", "ref"), None)),
        check_vma=False,
    )
```

```python
import math

import jax
import jax.numpy as jnp
from jax import lax
from jax.experimental import pallas as pl
from jax.experimental.pallas import tpu as pltpu
from jax.sharding import PartitionSpec as P

MESH = pl.DeviceIdType.MESH
F32, BF16 = jnp.float32, jnp.bfloat16
LOG2E = math.log2(math.e)

NDOM, NREFD = 16, 16
ROWS, WIDTH = 32, 128
BLOCK = ROWS * NREFD
REFS = 1024
STEP = 0.5
COUNT_P, COUNT_R = 8192, 16384

DOM_SLOTS = [(0, 0), (0, 1), (1, 0), (7, 0), (1, 1), (7, 1), (2, 0), (6, 0)]
DOM_SLOTS += [(2, 1), (6, 1), (3, 0), (5, 0), (3, 1), (5, 1), (4, 0), (4, 1)]
REF_SLOTS = [(0, 0, 0), (0, 0, 1)] + [(0, y, c) for y in (1, 3, 2) for c in (0, 1)]
REF_SLOTS += [(1, y, c) for y in (0, 1, 3, 2) for c in (0, 1)]


def dom_partner(d, slot):
    dz, dx = DOM_SLOTS[slot]
    return ((d // 2 + dz) % 8) * 2 + (d % 2 + dx) % 2


def ref_partner(r, slot):
    dx, dy, dc = REF_SLOTS[slot]
    return ((r // 8 + dx) % 2) * 8 + (((r // 2) % 4 + dy) % 4) * 2 + (r % 2 + dc) % 2


def dom_back(slot):
    dz, dx = DOM_SLOTS[slot]
    return DOM_SLOTS.index((-dz % 8, dx))


def ref_back(slot):
    dx, dy, dc = REF_SLOTS[slot]
    return REF_SLOTS.index((dx, -dy % 4, dc))


def split(x):
    hi = x.astype(BF16)
    return hi, (x - hi.astype(F32)).astype(BF16)


def extra(norm, ones_first):
    lane = lax.broadcasted_iota(jnp.int32, (norm.shape[0], 128), 1)
    n1 = norm.astype(BF16).astype(F32)
    rest = norm - n1
    n2 = rest.astype(BF16).astype(F32)
    n3 = rest - n2
    at, one = (3, 0) if ones_first else (0, 3)
    out = jnp.where((lane >= one) & (lane < one + 3), 1.0, 0.0)
    out = jnp.where(lane == at, n1, out)
    out = jnp.where(lane == at + 1, n2, out)
    return jnp.where(lane == at + 2, n3, out).astype(BF16)


def source_operand(x):
    hi, lo = split(x)
    norm = jnp.sum(x * x, axis=1, keepdims=True) * (-0.5 * LOG2E)
    return jnp.concatenate([hi, lo, hi, extra(norm, False)], axis=1)


def target_operand(x):
    hi, lo = split(x * LOG2E)
    norm = jnp.sum(x * x, axis=1, keepdims=True) * (-0.5 * LOG2E)
    return jnp.concatenate([hi, hi, lo, extra(norm, True)], axis=1)


def pair_terms(a, s_ref, start, size):
    src = s_ref[pl.ds(start, size), :]
    expo = lax.dot_general(a, src, (((1,), (1,)), ((), ())), preferred_element_type=F32)
    w = jnp.exp2(expo)
    w_hi = w.astype(BF16)
    w_lo = (w - w_hi.astype(F32)).astype(BF16)
    one = jnp.dot(w_hi, src[:, :256], preferred_element_type=F32)
    two = jnp.dot(w_lo, src[:, :128], preferred_element_type=F32)
    sums = w[:, :128]
    for c in range(1, size // 128):
        sums = sums + w[:, c * 128 : (c + 1) * 128]
    return one[:, :128] + one[:, 128:] + two, sums


def kernel(
    p_hbm, r_hbm, out_ref,
    p_v, r_v, xs, aop, rop, sop, grad, lanes, part, own, g_b, g_a, rs,
    in_sem, b_send, b_recv, a_send, a_recv, rs_send, rs_recv,
):
    d, r = lax.axis_index("dom"), lax.axis_index("ref")
    mine = pl.ds(pl.multiple_of(r * ROWS, ROWS), ROWS)
    copy_own = pltpu.make_async_copy(p_hbm.at[mine], own.at[0], in_sem.at[0])
    copy_p = pltpu.make_async_copy(p_hbm, p_v, in_sem.at[1])
    copy_r = pltpu.make_async_copy(r_hbm, r_v, in_sem.at[2])
    barrier = pltpu.get_barrier_semaphore()
    for slot in range(15, 0, -1):
        device = {"dom": dom_partner(d, slot)}
        pl.semaphore_signal(barrier, 1, device_id=device, device_id_type=MESH)
    copy_own.start()
    copy_p.start()
    copy_r.start()
    for slot in range(15, 0, -1):
        device = {"ref": ref_partner(r, slot)}
        pl.semaphore_signal(barrier, 1, device_id=device, device_id_type=MESH)

    def dom_copy(src, dst, send, recv, slot):
        to = dom_back(slot)
        return pltpu.make_async_remote_copy(
            src, dst.at[to], send, recv.at[to // 8],
            device_id={"dom": dom_partner(d, slot)}, device_id_type=MESH,
        )

    def ref_copy(src, dst, send, recv, slot):
        to = ref_back(slot)
        return pltpu.make_async_remote_copy(
            src, dst.at[to], send, recv.at[to // 8],
            device_id={"ref": ref_partner(r, slot)}, device_id_type=MESH,
        )

    def send_b(step):
        first = [s for x in (1, 0) for s in range(15, 0, -1) if DOM_SLOTS[s][1] == x]
        for slot in range(15, 0, -1) if step else first:
            dom_copy(own.at[step], g_b.at[step], b_send.at[step], b_recv.at[step], slot).start()

    def send_a():
        for slot in range(15, 0, -1):
            ref_copy(own.at[1], g_a, a_send, a_recv, slot).start()

    def send_rs(step, slots):
        for slot in slots:
            src = part.at[step, slot]
            ref_copy(src, rs.at[step], rs_send.at[step], rs_recv.at[step], slot).start()

    def arrived(dst, recv, half):
        pieces = dst.at[pl.ds(1, 7)] if half == 0 else dst.at[pl.ds(8, 8)]
        pltpu.make_async_copy(pieces, pieces, recv.at[half]).wait()

    def sent(dst, send):
        pieces = dst.at[pl.ds(1, 15)]
        pltpu.make_async_copy(pieces, pieces, send).wait()

    near, far = pl.ds(0, 256), pl.ds(256, 256)

    def refs_part(rows):
        a = aop[rows, :]
        acc, sums = pair_terms(a, rop, 0, 1024)
        grad[rows, :] = -0.5 * acc
        lanes[rows, :] = -0.5 * sums

    def particles_part(step, rows):
        acc, sums = pair_terms(aop[rows, :], sop, 0, 512)
        total = jnp.sum(lanes[rows, :] + sums, axis=1, keepdims=True)
        value = grad[rows, :] + acc - total * xs[rows, :]
        count = rows.size // ROWS
        part[step, pl.ds(rows.start // ROWS, count)] = value.reshape(count, ROWS, WIDTH)

    def prep_b(step, rows):
        pieces = g_b[step, pl.ds(rows.start // ROWS, 8)]
        sop[rows, :] = source_operand(pieces.reshape(256, WIDTH))

    def finish(step):
        arrived(g_b.at[step], b_recv.at[step], 1)
        arrived(g_b.at[step], b_recv.at[step], 0)
        for rows in (far, near):
            prep_b(step, rows)
        particles_part(step, far)
        send_rs(step, range(15, 7, -1))
        particles_part(step, near)
        send_rs(step, range(7, 0, -1))
        arrived(rs.at[step], rs_recv.at[step], 0)
        arrived(rs.at[step], rs_recv.at[step], 1)
        total = part[step, 0]
        for slot in range(1, 16):
            total = total + rs[step, slot]
        return total * (STEP / COUNT_P)

    copy_own.wait()
    pl.semaphore_wait(barrier, 30)
    send_b(0)
    start = own[0]
    g_b[0, 0] = start
    copy_p.wait()
    for slot in range(16):
        rows = pl.ds(pl.multiple_of(ref_partner(r, slot) * ROWS, ROWS), ROWS)
        xs[pl.ds(slot * ROWS, ROWS), :] = p_v[rows, :]
    for rows in (near, far):
        aop[rows, :] = target_operand(xs[rows, :])
    copy_r.wait()
    for i in range(4):
        rows = pl.ds(i * 256, 256)
        rop[rows, :] = source_operand(r_v[rows, :])
    for rows in (near, far):
        refs_part(rows)
    now = start - finish(0)

    own[1] = now
    send_a()
    send_b(1)
    g_b[1, 0] = now
    g_a[0] = now
    for half, rows in ((0, near), (1, far)):
        arrived(g_a, a_recv, half)
        xs[rows, :] = g_a[pl.ds(half * 8, 8)].reshape(256, WIDTH)
        aop[rows, :] = target_operand(xs[rows, :])
        refs_part(rows)
    delta = finish(1)
    out_ref[0] = start
    out_ref[1] = now
    out_ref[2] = delta
    for step in range(2):
        sent(g_b.at[step], b_send.at[step])
        sent(rs.at[step], rs_send.at[step])
    sent(g_a, a_send)


def on_device(particles, references):
    inputs = [pltpu.with_memory_space_constraint(x, pltpu.HBM) for x in (particles, references)]
    out = pl.pallas_call(
        kernel,
        out_shape=jax.ShapeDtypeStruct((3, ROWS, WIDTH), F32),
        in_specs=[pl.BlockSpec(memory_space=pltpu.HBM)] * 2,
        out_specs=pl.BlockSpec(memory_space=pltpu.VMEM),
        scratch_shapes=[
            pltpu.VMEM((BLOCK, WIDTH), F32),
            pltpu.VMEM((REFS, WIDTH), F32),
            pltpu.VMEM((BLOCK, WIDTH), F32),
            pltpu.VMEM((BLOCK, 512), BF16),
            pltpu.VMEM((REFS, 512), BF16),
            pltpu.VMEM((NDOM * ROWS, 512), BF16),
            pltpu.VMEM((BLOCK, WIDTH), F32),
            pltpu.VMEM((BLOCK, WIDTH), F32),
            pltpu.VMEM((2, NREFD, ROWS, WIDTH), F32),
            pltpu.VMEM((2, ROWS, WIDTH), F32),
            pltpu.VMEM((2, NDOM, ROWS, WIDTH), F32),
            pltpu.VMEM((NREFD, ROWS, WIDTH), F32),
            pltpu.VMEM((2, NREFD, ROWS, WIDTH), F32),
            pltpu.SemaphoreType.DMA((3,)),
            pltpu.SemaphoreType.DMA((2,)),
            pltpu.SemaphoreType.DMA((2, 2)),
            pltpu.SemaphoreType.DMA(()),
            pltpu.SemaphoreType.DMA((2,)),
            pltpu.SemaphoreType.DMA((2,)),
            pltpu.SemaphoreType.DMA((2, 2)),
        ],
        compiler_params=pltpu.CompilerParams(
            collective_id=0, has_side_effects=True, vmem_limit_bytes=24 << 20
        ),
        name="flow",
    )(*inputs)
    moved = out[1] - out[2]
    return moved, (moved - out[0]) * (1.0 / STEP)


def solution(mesh):
    return jax.shard_map(
        on_device,
        mesh=mesh,
        in_specs=(P("dom", None), P("ref", None)),
        out_specs=(P(("dom", "ref"), None), P(("dom", "ref"), None)),
        check_vma=False,
    )
```

```python
import math

import jax
import jax.numpy as jnp
from jax import lax
from jax.experimental import pallas as pl
from jax.experimental.pallas import tpu as pltpu
from jax.sharding import PartitionSpec as P

MESH = pl.DeviceIdType.MESH
F32, BF16 = jnp.float32, jnp.bfloat16
LOG2E = math.log2(math.e)

NDOM, NREFD = 16, 16
ROWS, WIDTH = 32, 128
BLOCK = ROWS * NREFD
REFS = 1024
STEP = 0.5
COUNT_P, COUNT_R = 8192, 16384

DOM_SLOTS = [(0, 0), (0, 1), (1, 0), (7, 0), (1, 1), (7, 1), (2, 0), (6, 0)]
DOM_SLOTS += [(2, 1), (6, 1), (3, 0), (5, 0), (3, 1), (5, 1), (4, 0), (4, 1)]
REF_SLOTS = [(0, 0, 0), (0, 0, 1)] + [(0, y, c) for y in (1, 3, 2) for c in (0, 1)]
REF_SLOTS += [(1, y, c) for y in (0, 1, 3, 2) for c in (0, 1)]


def dom_partner(d, slot):
    dz, dx = DOM_SLOTS[slot]
    return ((d // 2 + dz) % 8) * 2 + (d % 2 + dx) % 2


def ref_partner(r, slot):
    dx, dy, dc = REF_SLOTS[slot]
    return ((r // 8 + dx) % 2) * 8 + (((r // 2) % 4 + dy) % 4) * 2 + (r % 2 + dc) % 2


def dom_back(slot):
    dz, dx = DOM_SLOTS[slot]
    return DOM_SLOTS.index((-dz % 8, dx))


def ref_back(slot):
    dx, dy, dc = REF_SLOTS[slot]
    return REF_SLOTS.index((dx, -dy % 4, dc))


def split(x):
    hi = x.astype(BF16)
    return hi, (x - hi.astype(F32)).astype(BF16)


def extra(norm, ones_first):
    lane = lax.broadcasted_iota(jnp.int32, (norm.shape[0], 128), 1)
    n1 = norm.astype(BF16).astype(F32)
    rest = norm - n1
    n2 = rest.astype(BF16).astype(F32)
    n3 = rest - n2
    at, one = (3, 0) if ones_first else (0, 3)
    out = jnp.where((lane >= one) & (lane < one + 3), 1.0, 0.0)
    out = jnp.where(lane == at, n1, out)
    out = jnp.where(lane == at + 1, n2, out)
    return jnp.where(lane == at + 2, n3, out).astype(BF16)


def source_operand(x):
    hi, lo = split(x)
    norm = jnp.sum(x * x, axis=1, keepdims=True) * (-0.5 * LOG2E)
    return jnp.concatenate([hi, lo, hi, extra(norm, False)], axis=1)


def target_operand(x):
    hi, lo = split(x * LOG2E)
    norm = jnp.sum(x * x, axis=1, keepdims=True) * (-0.5 * LOG2E)
    return jnp.concatenate([hi, hi, lo, extra(norm, True)], axis=1)


def pair_terms(a, s_ref, start, size):
    src = s_ref[pl.ds(start, size), :]
    expo = lax.dot_general(a, src, (((1,), (1,)), ((), ())), preferred_element_type=F32)
    w = jnp.exp2(expo)
    w_hi = w.astype(BF16)
    w_lo = (w - w_hi.astype(F32)).astype(BF16)
    one = jnp.dot(w_hi, src[:, :256], preferred_element_type=F32)
    two = jnp.dot(w_lo, src[:, :128], preferred_element_type=F32)
    sums = w[:, :128]
    for c in range(1, size // 128):
        sums = sums + w[:, c * 128 : (c + 1) * 128]
    return one[:, :128] + one[:, 128:] + two, sums


def kernel(
    p_hbm, r_hbm, out_ref,
    p_v, r_v, xs, aop, rop, sop, grad, lanes, part, own, g_b, g_a, rs,
    in_sem, b_send, b_recv, a_send, a_recv, rs_send, rs_recv,
):
    d, r = lax.axis_index("dom"), lax.axis_index("ref")
    mine = pl.ds(pl.multiple_of(r * ROWS, ROWS), ROWS)
    copy_own = pltpu.make_async_copy(p_hbm.at[mine], own.at[0], in_sem.at[0])
    copy_p = pltpu.make_async_copy(p_hbm, p_v, in_sem.at[1])
    copy_r = pltpu.make_async_copy(r_hbm, r_v, in_sem.at[2])
    copy_own.start()
    copy_p.start()
    copy_r.start()

    barrier = pltpu.get_barrier_semaphore()
    for slot in range(15, 0, -1):
        device = {"dom": dom_partner(d, slot)}
        pl.semaphore_signal(barrier, 1, device_id=device, device_id_type=MESH)
    for slot in range(15, 0, -1):
        device = {"ref": ref_partner(r, slot)}
        pl.semaphore_signal(barrier, 1, device_id=device, device_id_type=MESH)

    def dom_copy(src, dst, send, recv, slot):
        to = dom_back(slot)
        return pltpu.make_async_remote_copy(
            src, dst.at[to], send, recv.at[to // 8],
            device_id={"dom": dom_partner(d, slot)}, device_id_type=MESH,
        )

    def ref_copy(src, dst, send, recv, slot):
        to = ref_back(slot)
        return pltpu.make_async_remote_copy(
            src, dst.at[to], send, recv.at[to // 8],
            device_id={"ref": ref_partner(r, slot)}, device_id_type=MESH,
        )

    def send_b(step):
        first = [s for x in (1, 0) for s in range(15, 0, -1) if DOM_SLOTS[s][1] == x]
        for slot in range(15, 0, -1) if step else first:
            dom_copy(own.at[step], g_b.at[step], b_send.at[step], b_recv.at[step], slot).start()

    flip = {10: 12, 11: 13, 12: 10, 13: 11, 2: 4, 3: 5, 4: 2, 5: 3}

    def by_core(slots, send):
        @pl.when(r % 2 == 0)
        def _():
            for slot in slots:
                send(slot)

        @pl.when(r % 2 == 1)
        def _():
            for slot in slots:
                send(flip.get(slot, slot))

    def send_a():
        by_core(range(15, 0, -1), lambda slot: ref_copy(own.at[1], g_a, a_send, a_recv, slot).start())

    def send_rs(step, slots):
        sems = rs_send.at[step], rs_recv.at[step]
        by_core(slots, lambda slot: ref_copy(part.at[step, slot], rs.at[step], *sems, slot).start())

    def arrived(dst, recv, half):
        pieces = dst.at[pl.ds(1, 7)] if half == 0 else dst.at[pl.ds(8, 8)]
        pltpu.make_async_copy(pieces, pieces, recv.at[half]).wait()

    def sent(dst, send):
        pieces = dst.at[pl.ds(1, 15)]
        pltpu.make_async_copy(pieces, pieces, send).wait()

    near, far = pl.ds(0, 256), pl.ds(256, 256)

    def refs_part(rows):
        a = aop[rows, :]
        acc, sums = pair_terms(a, rop, 0, 512)
        acc2, sums2 = pair_terms(a, rop, 512, 512)
        grad[rows, :] = -0.5 * (acc + acc2)
        lanes[rows, :] = -0.5 * (sums + sums2)

    def particles_part(step, rows):
        acc, sums = pair_terms(aop[rows, :], sop, 0, 512)
        total = jnp.sum(lanes[rows, :] + sums, axis=1, keepdims=True)
        value = grad[rows, :] + acc - total * xs[rows, :]
        count = rows.size // ROWS
        part[step, pl.ds(rows.start // ROWS, count)] = value.reshape(count, ROWS, WIDTH)

    def prep_b(step, rows):
        pieces = g_b[step, pl.ds(rows.start // ROWS, 8)]
        sop[rows, :] = source_operand(pieces.reshape(256, WIDTH))

    def finish(step):
        arrived(g_b.at[step], b_recv.at[step], 1)
        prep_b(step, far)
        arrived(g_b.at[step], b_recv.at[step], 0)
        prep_b(step, near)
        particles_part(step, far)
        send_rs(step, range(15, 7, -1))
        particles_part(step, near)
        send_rs(step, range(7, 0, -1))
        arrived(rs.at[step], rs_recv.at[step], 0)
        arrived(rs.at[step], rs_recv.at[step], 1)
        total = part[step, 0]
        for slot in range(1, 16):
            total = total + rs[step, slot]
        return total * (STEP / COUNT_P)

    copy_own.wait()
    pl.semaphore_wait(barrier, 30)
    send_b(0)
    start = own[0]
    g_b[0, 0] = start
    copy_p.wait()
    for slot in range(16):
        rows = pl.ds(pl.multiple_of(ref_partner(r, slot) * ROWS, ROWS), ROWS)
        xs[pl.ds(slot * ROWS, ROWS), :] = p_v[rows, :]
    for rows in (near, far):
        aop[rows, :] = target_operand(xs[rows, :])
    copy_r.wait()
    for i in range(4):
        rows = pl.ds(i * 256, 256)
        rop[rows, :] = source_operand(r_v[rows, :])
    for rows in (near, far):
        refs_part(rows)
    now = start - finish(0)

    own[1] = now
    send_a()
    send_b(1)
    g_b[1, 0] = now
    g_a[0] = now
    for half, rows in ((0, near), (1, far)):
        arrived(g_a, a_recv, half)
        xs[rows, :] = g_a[pl.ds(half * 8, 8)].reshape(256, WIDTH)
        aop[rows, :] = target_operand(xs[rows, :])
        refs_part(rows)
    delta = finish(1)
    out_ref[0] = start
    out_ref[1] = now
    out_ref[2] = delta
    for step in range(2):
        sent(g_b.at[step], b_send.at[step])
        sent(rs.at[step], rs_send.at[step])
    sent(g_a, a_send)


def on_device(particles, references):
    inputs = [pltpu.with_memory_space_constraint(x, pltpu.HBM) for x in (particles, references)]
    out = pl.pallas_call(
        kernel,
        out_shape=jax.ShapeDtypeStruct((3, ROWS, WIDTH), F32),
        in_specs=[pl.BlockSpec(memory_space=pltpu.HBM)] * 2,
        out_specs=pl.BlockSpec(memory_space=pltpu.VMEM),
        scratch_shapes=[
            pltpu.VMEM((BLOCK, WIDTH), F32),
            pltpu.VMEM((REFS, WIDTH), F32),
            pltpu.VMEM((BLOCK, WIDTH), F32),
            pltpu.VMEM((BLOCK, 512), BF16),
            pltpu.VMEM((REFS, 512), BF16),
            pltpu.VMEM((NDOM * ROWS, 512), BF16),
            pltpu.VMEM((BLOCK, WIDTH), F32),
            pltpu.VMEM((BLOCK, WIDTH), F32),
            pltpu.VMEM((2, NREFD, ROWS, WIDTH), F32),
            pltpu.VMEM((2, ROWS, WIDTH), F32),
            pltpu.VMEM((2, NDOM, ROWS, WIDTH), F32),
            pltpu.VMEM((NREFD, ROWS, WIDTH), F32),
            pltpu.VMEM((2, NREFD, ROWS, WIDTH), F32),
            pltpu.SemaphoreType.DMA((3,)),
            pltpu.SemaphoreType.DMA((2,)),
            pltpu.SemaphoreType.DMA((2, 2)),
            pltpu.SemaphoreType.DMA(()),
            pltpu.SemaphoreType.DMA((2,)),
            pltpu.SemaphoreType.DMA((2,)),
            pltpu.SemaphoreType.DMA((2, 2)),
        ],
        compiler_params=pltpu.CompilerParams(
            collective_id=0, has_side_effects=True, vmem_limit_bytes=24 << 20
        ),
        name="flow",
    )(*inputs)
    moved = out[1] - out[2]
    return moved, (moved - out[0]) * (1.0 / STEP)


def solution(mesh):
    return jax.shard_map(
        on_device,
        mesh=mesh,
        in_specs=(P("dom", None), P("ref", None)),
        out_specs=(P(("dom", "ref"), None), P(("dom", "ref"), None)),
        check_vma=False,
    )
```

```python
import math

import jax
import jax.numpy as jnp
from jax import lax
from jax.experimental import pallas as pl
from jax.experimental.pallas import tpu as pltpu
from jax.sharding import PartitionSpec as P

MESH = pl.DeviceIdType.MESH
F32, BF16 = jnp.float32, jnp.bfloat16
LOG2E = math.log2(math.e)

NDOM, NREFD = 16, 16
ROWS, WIDTH = 32, 128
BLOCK = ROWS * NREFD
REFS = 1024
STEP = 0.5
COUNT_P, COUNT_R = 8192, 16384

DOM_SLOTS = [(0, 0), (0, 1), (1, 0), (7, 0), (1, 1), (7, 1), (2, 0), (6, 0)]
DOM_SLOTS += [(2, 1), (6, 1), (3, 0), (5, 0), (3, 1), (5, 1), (4, 0), (4, 1)]
REF_SLOTS = [(0, 0, 0), (0, 0, 1)] + [(0, y, c) for y in (1, 3, 2) for c in (0, 1)]
REF_SLOTS += [(1, y, c) for y in (0, 1, 3, 2) for c in (0, 1)]


def dom_partner(d, slot):
    dz, dx = DOM_SLOTS[slot]
    return ((d // 2 + dz) % 8) * 2 + (d % 2 + dx) % 2


def ref_partner(r, slot):
    dx, dy, dc = REF_SLOTS[slot]
    return ((r // 8 + dx) % 2) * 8 + (((r // 2) % 4 + dy) % 4) * 2 + (r % 2 + dc) % 2


def dom_back(slot):
    dz, dx = DOM_SLOTS[slot]
    return DOM_SLOTS.index((-dz % 8, dx))


def ref_back(slot):
    dx, dy, dc = REF_SLOTS[slot]
    return REF_SLOTS.index((dx, -dy % 4, dc))


def split(x):
    hi = x.astype(BF16)
    return hi, (x - hi.astype(F32)).astype(BF16)


def extra(norm, ones_first):
    lane = lax.broadcasted_iota(jnp.int32, (norm.shape[0], 128), 1)
    n1 = norm.astype(BF16).astype(F32)
    rest = norm - n1
    n2 = rest.astype(BF16).astype(F32)
    n3 = rest - n2
    at, one = (3, 0) if ones_first else (0, 3)
    out = jnp.where((lane >= one) & (lane < one + 3), 1.0, 0.0)
    out = jnp.where(lane == at, n1, out)
    out = jnp.where(lane == at + 1, n2, out)
    return jnp.where(lane == at + 2, n3, out).astype(BF16)


def source_operand(x):
    hi, lo = split(x)
    norm = jnp.sum(x * x, axis=1, keepdims=True) * (-0.5 * LOG2E)
    return jnp.concatenate([hi, lo, hi, extra(norm, False)], axis=1)


def target_operand(x):
    hi, lo = split(x * LOG2E)
    norm = jnp.sum(x * x, axis=1, keepdims=True) * (-0.5 * LOG2E)
    return jnp.concatenate([hi, hi, lo, extra(norm, True)], axis=1)


def pair_terms(a, s_ref, start, size):
    src = s_ref[pl.ds(start, size), :]
    expo = lax.dot_general(a, src, (((1,), (1,)), ((), ())), preferred_element_type=F32)
    w = jnp.exp2(expo)
    w_hi = w.astype(BF16)
    w_lo = (w - w_hi.astype(F32)).astype(BF16)
    one = jnp.dot(w_hi, src[:, :256], preferred_element_type=F32)
    two = jnp.dot(w_lo, src[:, :128], preferred_element_type=F32)
    sums = w[:, :128]
    for c in range(1, size // 128):
        sums = sums + w[:, c * 128 : (c + 1) * 128]
    return one[:, :128] + one[:, 128:] + two, sums


def kernel(
    p_hbm, r_hbm, out_ref,
    p_v, r_v, xs, aop, rop, sop, grad, lanes, part, own, g_b, g_a, rs,
    in_sem, b_send, b_recv, a_send, a_recv, rs_send, rs_recv,
):
    d, r = lax.axis_index("dom"), lax.axis_index("ref")
    mine = pl.ds(pl.multiple_of(r * ROWS, ROWS), ROWS)
    copy_own = pltpu.make_async_copy(p_hbm.at[mine], own.at[0], in_sem.at[0])
    copy_p = pltpu.make_async_copy(p_hbm, p_v, in_sem.at[1])
    copy_r = pltpu.make_async_copy(r_hbm, r_v, in_sem.at[2])
    copy_own.start()
    copy_p.start()
    copy_r.start()

    barrier = pltpu.get_barrier_semaphore()
    for slot in range(15, 0, -1):
        device = {"dom": dom_partner(d, slot)}
        pl.semaphore_signal(barrier, 1, device_id=device, device_id_type=MESH)
    for slot in range(15, 0, -1):
        device = {"ref": ref_partner(r, slot)}
        pl.semaphore_signal(barrier, 1, device_id=device, device_id_type=MESH)

    def dom_copy(src, dst, send, recv, slot):
        to = dom_back(slot)
        return pltpu.make_async_remote_copy(
            src, dst.at[to], send, recv.at[to // 8],
            device_id={"dom": dom_partner(d, slot)}, device_id_type=MESH,
        )

    def ref_copy(src, dst, send, recv, slot):
        to = ref_back(slot)
        return pltpu.make_async_remote_copy(
            src, dst.at[to], send, recv.at[to // 8],
            device_id={"ref": ref_partner(r, slot)}, device_id_type=MESH,
        )

    def send_b(step):
        first = [s for x in (1, 0) for s in range(15, 0, -1) if DOM_SLOTS[s][1] == x]
        for slot in range(15, 0, -1) if step else first:
            dom_copy(own.at[step], g_b.at[step], b_send.at[step], b_recv.at[step], slot).start()

    flip = {10: 12, 11: 13, 12: 10, 13: 11, 2: 4, 3: 5, 4: 2, 5: 3}

    def by_core(slots, send):
        @pl.when(r % 2 == 0)
        def _():
            for slot in slots:
                send(slot)

        @pl.when(r % 2 == 1)
        def _():
            for slot in slots:
                send(flip.get(slot, slot))

    def send_a():
        by_core(range(15, 0, -1), lambda slot: ref_copy(own.at[1], g_a, a_send, a_recv, slot).start())

    def send_rs(step, slots):
        sems = rs_send.at[step], rs_recv.at[step]
        by_core(slots, lambda slot: ref_copy(part.at[step, slot], rs.at[step], *sems, slot).start())

    def arrived(dst, recv, half):
        pieces = dst.at[pl.ds(1, 7)] if half == 0 else dst.at[pl.ds(8, 8)]
        pltpu.make_async_copy(pieces, pieces, recv.at[half]).wait()

    def sent(dst, send):
        pieces = dst.at[pl.ds(1, 15)]
        pltpu.make_async_copy(pieces, pieces, send).wait()

    near, far = pl.ds(0, 256), pl.ds(256, 256)

    def refs_part(rows):
        a = aop[rows, :]
        acc, sums = pair_terms(a, rop, 0, 1024)
        grad[rows, :] = -0.5 * acc
        lanes[rows, :] = -0.5 * sums

    def particles_part(step, rows):
        acc, sums = pair_terms(aop[rows, :], sop, 0, 512)
        total = jnp.sum(lanes[rows, :] + sums, axis=1, keepdims=True)
        value = grad[rows, :] + acc - total * xs[rows, :]
        count = rows.size // ROWS
        part[step, pl.ds(rows.start // ROWS, count)] = value.reshape(count, ROWS, WIDTH)

    def prep_b(step, rows):
        pieces = g_b[step, pl.ds(rows.start // ROWS, 8)]
        sop[rows, :] = source_operand(pieces.reshape(256, WIDTH))

    def finish(step):
        arrived(g_b.at[step], b_recv.at[step], 1)
        prep_b(step, far)
        arrived(g_b.at[step], b_recv.at[step], 0)
        prep_b(step, near)
        particles_part(step, far)
        send_rs(step, range(15, 7, -1))
        particles_part(step, near)
        send_rs(step, range(7, 0, -1))
        arrived(rs.at[step], rs_recv.at[step], 0)
        arrived(rs.at[step], rs_recv.at[step], 1)
        total = part[step, 0]
        for slot in range(1, 16):
            total = total + rs[step, slot]
        return total * (STEP / COUNT_P)

    copy_own.wait()
    pl.semaphore_wait(barrier, 30)
    send_b(0)
    start = own[0]
    g_b[0, 0] = start
    copy_p.wait()
    for slot in range(16):
        rows = pl.ds(pl.multiple_of(ref_partner(r, slot) * ROWS, ROWS), ROWS)
        xs[pl.ds(slot * ROWS, ROWS), :] = p_v[rows, :]
    for rows in (near, far):
        aop[rows, :] = target_operand(xs[rows, :])
    copy_r.wait()
    for i in range(4):
        rows = pl.ds(i * 256, 256)
        rop[rows, :] = source_operand(r_v[rows, :])
    for rows in (near, far):
        refs_part(rows)
    now = start - finish(0)

    own[1] = now
    send_a()
    send_b(1)
    g_b[1, 0] = now
    g_a[0] = now
    for half, rows in ((0, near), (1, far)):
        arrived(g_a, a_recv, half)
        xs[rows, :] = g_a[pl.ds(half * 8, 8)].reshape(256, WIDTH)
        aop[rows, :] = target_operand(xs[rows, :])
        refs_part(rows)
    delta = finish(1)
    out_ref[0] = start
    out_ref[1] = now
    out_ref[2] = delta
    for step in range(2):
        sent(g_b.at[step], b_send.at[step])
        sent(rs.at[step], rs_send.at[step])
    sent(g_a, a_send)


def on_device(particles, references):
    inputs = [pltpu.with_memory_space_constraint(x, pltpu.HBM) for x in (particles, references)]
    out = pl.pallas_call(
        kernel,
        out_shape=jax.ShapeDtypeStruct((3, ROWS, WIDTH), F32),
        in_specs=[pl.BlockSpec(memory_space=pltpu.HBM)] * 2,
        out_specs=pl.BlockSpec(memory_space=pltpu.VMEM),
        scratch_shapes=[
            pltpu.VMEM((BLOCK, WIDTH), F32),
            pltpu.VMEM((REFS, WIDTH), F32),
            pltpu.VMEM((BLOCK, WIDTH), F32),
            pltpu.VMEM((BLOCK, 512), BF16),
            pltpu.VMEM((REFS, 512), BF16),
            pltpu.VMEM((NDOM * ROWS, 512), BF16),
            pltpu.VMEM((BLOCK, WIDTH), F32),
            pltpu.VMEM((BLOCK, WIDTH), F32),
            pltpu.VMEM((2, NREFD, ROWS, WIDTH), F32),
            pltpu.VMEM((2, ROWS, WIDTH), F32),
            pltpu.VMEM((2, NDOM, ROWS, WIDTH), F32),
            pltpu.VMEM((NREFD, ROWS, WIDTH), F32),
            pltpu.VMEM((2, NREFD, ROWS, WIDTH), F32),
            pltpu.SemaphoreType.DMA((3,)),
            pltpu.SemaphoreType.DMA((2,)),
            pltpu.SemaphoreType.DMA((2, 2)),
            pltpu.SemaphoreType.DMA(()),
            pltpu.SemaphoreType.DMA((2,)),
            pltpu.SemaphoreType.DMA((2,)),
            pltpu.SemaphoreType.DMA((2, 2)),
        ],
        compiler_params=pltpu.CompilerParams(
            collective_id=0, has_side_effects=True, vmem_limit_bytes=24 << 20
        ),
        name="flow",
    )(*inputs)
    moved = out[1] - out[2]
    return moved, (moved - out[0]) * (1.0 / STEP)


def solution(mesh):
    return jax.shard_map(
        on_device,
        mesh=mesh,
        in_specs=(P("dom", None), P("ref", None)),
        out_specs=(P(("dom", "ref"), None), P(("dom", "ref"), None)),
        check_vma=False,
    )
```
